128 devices in a mesh: row: 4 (over x), col: 8 (over z_lo, y), layer: 4 (over z_hi, core).
Axes of the slice: x: 4, y: 4, z: 4 (z_hi: 2, z_lo: 2; z = z_hi * 2 + z_lo), core: 2. Of those that a mesh axis runs over, the one named last changes fastest.
Arguments:
- a_blocks: float32 [4096, 4096], P('row', ('col', 'layer')), may hold values from -6 to 6
- mask_a: int32 [64, 64], P('row', ('col', 'layer')), may hold values from 0 to 1, as said below
- b_blocks: float32 [4096, 32768], P('row', ('col', 'layer')), may hold values from -0.25 to 0.25
- mask_b: int32 [64, 512], P('row', ('col', 'layer')), may hold values from 0 to 1
Outputs:
- product: float32 [4096, 32768], P('row', ('col', 'layer'))
The draws below stay inside these ranges and needn't reach their ends.
Inputs may be any that keep to these rules, and one draw needn't show every extreme that they name: Within one device's shard of mask_a (16 block rows by 2 inner block indices) at most 8 blocks are stored; the shard of the first 16 block rows and first 2 inner indices stores exactly 8.
All inputs are finite; a program needn't handle non-finite values.
Results may differ from the reference program's by a relative error of at most 0.00007.
Values sent between devices are 32-bit elements; how exact they have to be, the bound alone decides.
No kernel may reach another device: no remote copies, remote signals or barrier semaphores. Data moves between devices by JAX's collectives and lax.ppermute only.
A program may use at most 128 MiB of HBM per device.

```python
import jax
import jax.numpy as jnp
from jax import lax

BLOCK = 64
MB_DEV = 16
KB_DEV = 2
CAP_A = 8
MB = 64
KB = 64
NB = 512


def banded(key, height, width):
    rows = jnp.arange(height, dtype=jnp.int32)[:, None]
    cols = jnp.arange(width, dtype=jnp.int32)[None, :]
    dist = jnp.abs(cols * height - rows * width)
    near = dist <= max(height, width)
    rolls = jax.random.randint(key, (height, width), 0, 100)
    return jnp.where(near, rolls < 90, rolls < 12)


def draw_mask_a(key, part):
    key_band, key_order = jax.random.split(jax.random.fold_in(key, 11))
    chosen = banded(key_band, MB, KB)
    rows = jnp.arange(MB, dtype=jnp.int32)[:, None]
    cols = jnp.arange(KB, dtype=jnp.int32)[None, :]
    chosen = chosen | (rows < MB_DEV) & (cols < KB_DEV)
    order = jax.random.permutation(key_order, MB * KB).astype(jnp.int32).reshape(MB, KB)
    scores = jnp.where(chosen, order + 1, 0)
    groups = scores.reshape(MB // MB_DEV, MB_DEV, KB // KB_DEV, KB_DEV).transpose(0, 2, 1, 3)
    groups = groups.reshape(MB // MB_DEV, KB // KB_DEV, MB_DEV * KB_DEV)
    higher = jnp.sum((groups[..., None, :] > groups[..., :, None]).astype(jnp.int32), axis=-1)
    keeps = (groups > 0) & (higher < CAP_A)
    keeps = keeps.reshape(MB // MB_DEV, KB // KB_DEV, MB_DEV, KB_DEV).transpose(0, 2, 1, 3)
    return keeps.reshape(MB, KB).astype(jnp.int32)


def draw_mask_b(key, part):
    return banded(jax.random.fold_in(key, 23), KB, NB).astype(jnp.int32)


def steps_of(stream_key, extent, cuts, least, top_value):
    gain, own = 1.0, jax.random.fold_in(stream_key, 6)
    for position, shards_of in cuts:
        heights = jnp.exp(jax.random.uniform(jax.random.fold_in(own, position), (shards_of,), jnp.float32, least / len(cuts), top_value / len(cuts)))
        gain = gain * jnp.repeat(heights, extent[position] // shards_of).reshape([-1 if axis == position else 1 for axis in range(len(extent))])
    return gain


def normal_values(stream_key, dims, scale, reach, cuts=(), kind=jnp.bfloat16):
    array = jax.random.normal(stream_key, dims, jnp.float32) * scale
    if len(cuts) > 0:
        array = steps_of(stream_key, dims, cuts, -0.22, 0.18) * array
    return jnp.clip(array, min=-reach, max=reach).astype(kind)


def setup_inputs(seed: int = 0) -> dict:
    splits = jax.random.split(jax.random.key(seed), 5)
    a_blocks = normal_values(splits[0], (MB * BLOCK, KB * BLOCK), 1.0, 6.0, ((0, 4), (1, 32)), jnp.float32)
    mask_a = draw_mask_a(jax.random.fold_in(splits[4], 71), 0)
    b_blocks = normal_values(splits[2], (KB * BLOCK, NB * BLOCK), (KB * BLOCK // 8) ** -0.5, 0.25, ((0, 4), (1, 32)), jnp.float32)
    mask_b = draw_mask_b(jax.random.fold_in(splits[4], 71), 0)
    return dict(a_blocks=a_blocks, mask_a=mask_a, b_blocks=b_blocks, mask_b=mask_b)


def expand(mask):
    return jnp.repeat(jnp.repeat(mask, BLOCK, axis=0), BLOCK, axis=1).astype(jnp.float32)


def reference(a_blocks, mask_a, b_blocks, mask_b):
    a_masked = a_blocks * expand(mask_a)
    b_masked = b_blocks * expand(mask_b)
    return jnp.dot(a_masked, b_masked, precision=lax.Precision.HIGHEST, preferred_element_type=jnp.float32)
```

```python
import jax
import jax.numpy as jnp
from jax import lax
from jax.experimental import pallas as pl
from jax.experimental.pallas import tpu as pltpu
from jax.sharding import Mesh, PartitionSpec as P

BLOCK = 64
ROWS = 4
A_SLOTS = 8
A_TILES = A_SLOTS // 2
A_ROWS = 8 + A_TILES * BLOCK
B_SLOTS = 38
B_TILES = B_SLOTS // 2
B_ROWS = 8 + B_TILES * BLOCK
A_SHARDS = 32
A_PER_GROUP = 4
LHS_ROWS = (A_SHARDS * A_SLOTS + 4) * BLOCK
TAB = 512
TAB_START, TAB_COUNT, TAB_ROW, TAB_MOST = 0, 64, 128, 511
DUMP = 16
AXES = ("zl", "y", "zh", "core")
F32, BF16, I32 = jnp.float32, jnp.bfloat16, jnp.int32


def _lane(rows=1):
    return lax.broadcasted_iota(I32, (rows, 128), 1)


def _split_pair(left, right, odd_left, odd_right):
    a = jnp.where(odd_left == 1, pltpu.roll(left, 64, 1), left)
    b = jnp.where(odd_right == 1, right, pltpu.roll(right, 64, 1))
    return jnp.where(_lane(BLOCK) < 64, a, b)


def pack_kernel(round_ref, ma_ref, mb_ref, a_hbm, b_hbm, pa_ref, p0_ref, p1_ref, abuf, bbuf, ia, ib, sem):
    row = lax.axis_index("row")
    shard = lax.axis_index("zl") * 16 + lax.axis_index("y") * 4 + lax.axis_index("zh") * 2 + lax.axis_index("core")
    acopy = pltpu.make_async_copy(a_hbm, abuf, sem.at[0])
    bcopy = pltpu.make_async_copy(b_hbm, bbuf, sem.at[1])
    acopy.start()
    bcopy.start()

    for s in range(A_SLOTS):
        ia[s] = 0
    n = 0
    counts = []
    for k in range(2):
        for i in range(16):
            ia[n] = k * 16 + i
            n = n + ma_ref[i, k]
        counts.append(n)

    def clear(s, c):
        ib[s] = 0
        return c

    lax.fori_loop(0, 2 * B_SLOTS * 5, clear, 0, unroll=20)

    def scan_row(k, n):
        for j in range(16):
            ib[n] = k * 16 + j
            n = n + mb_ref[k, j]
        return n

    nb = lax.fori_loop(0, 16, scan_row, 0)
    ib[nb] = 0

    lane = _lane(8)
    acopy.wait()
    head = jnp.where(lane == 8, counts[0], jnp.where(lane == 9, counts[1] - counts[0], jnp.where(lane == 10, shard, 0)))
    for t in range(A_TILES):
        e0, e1 = ia[2 * t], ia[2 * t + 1]
        x0 = abuf[pl.ds(pl.multiple_of((e0 & 15) * BLOCK, BLOCK), BLOCK), :]
        x1 = abuf[pl.ds(pl.multiple_of((e1 & 15) * BLOCK, BLOCK), BLOCK), :]
        pa_ref[8 + t * BLOCK : 8 + (t + 1) * BLOCK, :] = _split_pair(x0, x1, e0 >> 4, e1 >> 4)
        head = jnp.where(lane == 2 * t, e0 & 15, jnp.where(lane == 2 * t + 1, e1 & 15, head))
    pa_ref[0:8, :] = head.astype(F32)

    bcopy.wait()
    first = round_ref[0] * (2 * B_SLOTS)
    for half, out in enumerate((p0_ref, p1_ref)):
        base = first + half * B_SLOTS

        def tile(t, head, base=base, out=out):
            s = base + 2 * t
            e0, e1 = ib[s], ib[s + 1]
            x0 = bbuf[pl.ds(pl.multiple_of((e0 >> 4) * BLOCK, BLOCK), BLOCK), pl.ds(pl.multiple_of(((e0 & 15) >> 1) * 128, 128), 128)]
            x1 = bbuf[pl.ds(pl.multiple_of((e1 >> 4) * BLOCK, BLOCK), BLOCK), pl.ds(pl.multiple_of(((e1 & 15) >> 1) * 128, 128), 128)]
            out[pl.ds(pl.multiple_of(8 + t * BLOCK, 8), BLOCK), :] = _split_pair(x0, x1, e0 & 1, e1 & 1)
            return jnp.where(lane == 2 * t, e0, jnp.where(lane == 2 * t + 1, e1, head))

        head = lax.fori_loop(0, B_TILES, tile, jnp.zeros((8, 128), I32), unroll=2)
        head = head + row * 256
        head = jnp.where(lane == 126, nb, head)
        head = jnp.where(lane == 127, jnp.clip(nb - base, 0, B_SLOTS), head)
        out[0:8, :] = head.astype(F32)


def pack(rnd, mask_a, mask_b, a, b):
    smem = pl.BlockSpec(memory_space=pltpu.SMEM)
    vmem = pl.BlockSpec(memory_space=pltpu.VMEM)
    hbm = pl.BlockSpec(memory_space=pl.ANY)
    return pl.pallas_call(
        pack_kernel,
        in_specs=[smem, smem, smem, hbm, hbm],
        out_specs=[vmem, vmem, vmem],
        out_shape=[
            jax.ShapeDtypeStruct((A_ROWS, 128), F32),
            jax.ShapeDtypeStruct((B_ROWS, 128), F32),
            jax.ShapeDtypeStruct((B_ROWS, 128), F32),
        ],
        scratch_shapes=[
            pltpu.VMEM(a.shape, F32),
            pltpu.VMEM(b.shape, F32),
            pltpu.SMEM((64,), I32),
            pltpu.SMEM((512,), I32),
            pltpu.SemaphoreType.DMA((2,)),
        ],
        compiler_params=pltpu.CompilerParams(vmem_limit_bytes=12 << 20),
        name="pack",
    )(rnd, mask_a, mask_b, a, b)


def product_kernel(*refs, n_half, first):
    n_a = A_SHARDS // A_PER_GROUP
    if first:
        a_hbm, refs = refs[:n_a], refs[n_a:]
    else:
        lhs_in, tab_in, c_in, refs = refs[0], refs[1], refs[2], refs[3:]
    b_hbm, refs = refs[:n_half], refs[n_half:]
    if first:
        c_out, lhs_out, tab, refs = refs[0], refs[1], refs[2], refs[3:]
        abuf, ahead, refs = refs[0], refs[1], refs[2:]
    else:
        c_out, most_out, refs = refs[0], refs[1], refs[2:]
        tab = tab_in
    lhs, c, bbuf, bhead, rhs, tk, tj, wt, ws, wn, sem = refs

    body_copies, head_copies = [], []
    for h in range(n_half):
        head_copies.append(pltpu.make_async_copy(b_hbm[h].at[pl.ds(0, 8), :], bhead.at[h], sem.at[0, h]))
        body_copies.append(pltpu.make_async_copy(b_hbm[h].at[pl.ds(8, B_ROWS - 8), :], bbuf.at[h], sem.at[1, h]))
    if first:
        a_copies, a_heads = [], []
        for g in range(n_a):
            a_copies.append(pltpu.make_async_copy(a_hbm[g], abuf.at[pl.ds(g * A_PER_GROUP * A_ROWS, A_PER_GROUP * A_ROWS), :], sem.at[2, g]))
            for q in range(A_PER_GROUP):
                a_heads.append(pltpu.make_async_copy(a_hbm[g].at[pl.ds(q * A_ROWS, 8), :], ahead.at[g * A_PER_GROUP + q], sem.at[3, g * A_PER_GROUP + q]))
        for copy in a_heads + a_copies:
            copy.start()
    else:
        lhs_copy = pltpu.make_async_copy(lhs_in, lhs, sem.at[2, 0])
        c_copy = pltpu.make_async_copy(c_in, c.at[pl.ds(0, 1024), :], sem.at[2, 1])
        lhs_copy.start()
        c_copy.start()
    for copy in head_copies + body_copies:
        copy.start()

    low = _lane(BLOCK) < 64

    def halves(x):
        hi = x.astype(BF16).astype(F32)
        return hi, x - hi

    if first:
        c[0:1024, :] = jnp.zeros((1024, 1024), F32)

        for g in range(n_a):
            for q in range(A_PER_GROUP):
                a_heads[g * A_PER_GROUP + q].wait()
            a_copies[g].wait()

            def shard(q, carry):
                head = ahead.at[q]
                n0 = head[0, 8].astype(I32)
                n1 = head[0, 9].astype(I32)
                at = head[0, 10].astype(I32)
                tab[TAB_START + 2 * at] = 8 * q
                tab[TAB_START + 2 * at + 1] = 8 * q + n0
                tab[TAB_COUNT + 2 * at] = n0
                tab[TAB_COUNT + 2 * at + 1] = n1
                for s in range(A_SLOTS):
                    tab[TAB_ROW + 8 * q + s] = head[0, s].astype(I32)
                for t in range(A_TILES):
                    x = abuf[pl.ds(pl.multiple_of(q * A_ROWS + 8 + t * BLOCK, 8), BLOCK), :]
                    swapped = pltpu.roll(x, 64, 1)
                    for p in range(2):
                        hi, lo = halves(jnp.where(low, x, swapped) if p == 0 else jnp.where(low, swapped, x))
                        lhs[pl.ds(pl.multiple_of((8 * q + 2 * t + p) * BLOCK, BLOCK), BLOCK), :] = jnp.where(low, hi, lo).astype(BF16)
                return carry

            lax.fori_loop(g * A_PER_GROUP, (g + 1) * A_PER_GROUP, shard, 0)
        for s in range(4):
            tab[TAB_ROW + A_SHARDS * A_SLOTS + s] = DUMP
        lhs_copy = pltpu.make_async_copy(lhs, lhs_out, sem.at[2, n_a])
        lhs_copy.start()

    most = I32(0) if first else tab[TAB_MOST]
    for h in range(n_half):
        head_copies[h].wait()
        body_copies[h].wait()
        head, body = bhead.at[h], bbuf.at[h]
        most = jnp.maximum(most, head[0, 126].astype(I32))
        n = head[0, 127].astype(I32)

        def unpack(s, carry):
            t, par, before, w, v = carry
            e = head[0, s].astype(I32)
            pair = e >> 1
            k = e >> 4
            new = pair != before
            new_k = k != (before >> 3)
            x = body[pl.ds(pl.multiple_of((s >> 1) * BLOCK, BLOCK), BLOCK), :]
            x = jnp.where(((s ^ e) & 1) == 1, pltpu.roll(x, 64, 1), x)
            v = jnp.where((_lane(BLOCK) >> 6) == (e & 1), x, jnp.where(new, 0.0, v))
            hi, lo = halves(v)
            t = t + new.astype(I32)
            rhs[pl.ds(pl.multiple_of(t * 128, 128), BLOCK), :] = hi.astype(BF16)
            rhs[pl.ds(pl.multiple_of(t * 128 + BLOCK, BLOCK), BLOCK), :] = lo.astype(BF16)
            par = jnp.where(new, jnp.where(new_k, 0, 1 - par), par)
            tk[t] = k
            tj[t] = pair & 7
            emit = jnp.logical_and(new, par == 0)
            nk = tab[TAB_COUNT + k]
            start = tab[TAB_START + k]
            wt[w] = t
            ws[w] = start
            wn[w] = jnp.minimum(nk, 4)
            w = w + jnp.logical_and(emit, nk > 0).astype(I32)
            wt[w] = t
            ws[w] = start + 4
            wn[w] = nk - 4
            w = w + jnp.logical_and(emit, nk > 4).astype(I32)
            return t, par, pair, w, v

        t, _, _, work, _ = lax.fori_loop(0, n, unpack, (I32(-1), I32(0), I32(-8), I32(0), jnp.zeros((BLOCK, 128), F32)))
        tk[t + 1] = -1
        tj[t + 1] = 0
        wt[work] = 0
        ws[work] = 0
        wn[work] = 0

        if not first and h == 0:
            lhs_copy.wait()
            c_copy.wait()

        def multiply(m, carry):
            results = []
            for u in range(2):
                w = 2 * m + u
                t, s = wt[w], ws[w]
                left = lhs[pl.ds(pl.multiple_of(s * BLOCK, BLOCK), 4 * BLOCK), :]
                cols = []
                for p in range(2):
                    tile = rhs[pl.ds(pl.multiple_of((t + p) * 128, 128), 128), :]
                    cols.append(jnp.concatenate([tile[:BLOCK], tile[:BLOCK], tile[BLOCK:], tile[BLOCK:]], axis=0))
                results.append(
                    jnp.dot(
                        jnp.concatenate([left, left], axis=1),
                        jnp.concatenate(cols, axis=1),
                        preferred_element_type=F32,
                    )
                )
            for u in range(2):
                w = 2 * m + u
                t, s, n = wt[w], ws[w], wn[w]
                both = tk[t + 1] == tk[t]
                for p in range(2):
                    col = pl.ds(pl.multiple_of(tj[t + p] * 128, 128), 128)
                    for q in range(4):
                        i = jnp.where(q < n, tab[TAB_ROW + s + q], DUMP)
                        if p == 1:
                            i = jnp.where(both, i, DUMP)
                        rows = pl.ds(pl.multiple_of(i * BLOCK, BLOCK), BLOCK)
                        c[rows, col] = c[rows, col] + results[u][q * BLOCK : (q + 1) * BLOCK, p * 128 : (p + 1) * 128]
            return carry

        lax.fori_loop(0, (work + 1) // 2, multiply, 0)

    if first:
        tab[TAB_MOST] = most
    else:
        most_out[0] = most
    out_copy = pltpu.make_async_copy(c.at[pl.ds(0, 1024), :], c_out, sem.at[3, A_SHARDS])
    out_copy.start()
    if first:
        lhs_copy.wait()
    out_copy.wait()


def product(a_parts, state, halves):
    first = state is None
    n_half = len(halves)
    smem = pl.BlockSpec(memory_space=pltpu.SMEM)
    hbm = pl.BlockSpec(memory_space=pl.ANY)
    c_type = jax.ShapeDtypeStruct((1024, 1024), F32)
    lhs_type = jax.ShapeDtypeStruct((LHS_ROWS, 128), BF16)
    tab_type = jax.ShapeDtypeStruct((TAB,), I32)
    scratch = [
        pltpu.VMEM((LHS_ROWS, 128), BF16),
        pltpu.VMEM((1024 + BLOCK, 1024), F32),
        pltpu.VMEM((n_half, B_ROWS - 8, 128), F32),
        pltpu.SMEM((n_half, 8, 128), F32),
        pltpu.VMEM(((B_SLOTS + 2) * 128, 128), BF16),
        pltpu.SMEM((64,), I32),
        pltpu.SMEM((64,), I32),
        pltpu.SMEM((128,), I32),
        pltpu.SMEM((128,), I32),
        pltpu.SMEM((128,), I32),
        pltpu.SemaphoreType.DMA((4, A_SHARDS + 1)),
    ]
    params = pltpu.CompilerParams(vmem_limit_bytes=24 << 20)
    if first:
        args = tuple(a_parts) + tuple(halves)
        scratch = [pltpu.VMEM((A_SHARDS * A_ROWS, 128), F32), pltpu.SMEM((A_SHARDS, 8, 128), F32)] + scratch
        in_specs = [hbm] * len(args)
        out_specs, out_shape, aliases = [hbm, hbm, smem], [c_type, lhs_type, tab_type], {}
    else:
        lhs, tab, c = state
        args = (lhs, tab, c) + tuple(halves)
        in_specs = [hbm, smem] + [hbm] * (len(args) - 2)
        out_specs, out_shape, aliases = [hbm, smem], [c_type, jax.ShapeDtypeStruct((1,), I32)], {2: 0}

    def kernel(*refs):
        product_kernel(*refs, n_half=n_half, first=first)

    return pl.pallas_call(
        kernel,
        in_specs=in_specs,
        out_specs=out_specs,
        out_shape=out_shape,
        input_output_aliases=aliases,
        scratch_shapes=scratch,
        compiler_params=params,
        name="product_first" if first else "product_more",
    )(*args)


def _flat(zl, y, zh, core):
    return ((zl * 4 + y) * 2 + zh) * 2 + core


def _turn(step, swapped):
    pairs = []
    for z in range(4):
        for y in range(4):
            for core in range(2):
                along_y = (core == 0) != swapped
                to_y, to_z = ((y + step) % 4, z) if along_y else (y, (z + step) % 4)
                pairs.append((_flat(z % 2, y, z // 2, core), _flat(to_z % 2, to_y, to_z // 2, core)))
    return pairs


def gather_a(packed):
    near = [packed] + [lax.ppermute(packed, AXES, _turn(s, False)) for s in (1, 3, 2)]
    group = jnp.concatenate(near, axis=0)
    mine = [group] + [lax.ppermute(group, AXES, _turn(s, True)) for s in (1, 3, 2)]
    other = [lax.ppermute(x, "core", [(0, 1), (1, 0)]) for x in mine]
    return mine + other


def ring_b(p0, p1):
    up = [(i, (i + 1) % ROWS) for i in range(ROWS)]
    down = [(i, (i - 1) % ROWS) for i in range(ROWS)]
    l0 = lax.ppermute(p0, "row", up)
    r1 = lax.ppermute(p1, "row", down)
    l1 = lax.ppermute(p1, "row", up)
    r0 = lax.ppermute(p0, "row", down)
    far0 = lax.ppermute(l0, "row", up)
    far1 = lax.ppermute(r1, "row", down)
    return (p0, p1, l0, r1, l1, r0), (far0, far1)


def shards(a_blocks, mask_a, b_blocks, mask_b):
    pa, p0, p1 = pack(jnp.zeros((1,), I32), mask_a, mask_b, a_blocks, b_blocks)
    near, far = ring_b(p0, p1)
    a_parts = gather_a(pa)
    c, lhs, tab = product(a_parts, None, near)
    c, most = product(None, (lhs, tab, c), far)
    most = most[0]

    def again(carry):
        r, c = carry
        _, p0, p1 = pack(r[None], mask_a, mask_b, a_blocks, b_blocks)
        near, far = ring_b(p0, p1)
        return r + 1, product(None, (lhs, tab, c), near + far)[0]

    return lax.while_loop(lambda carry: carry[0] * (2 * B_SLOTS) < most, again, (I32(1), c))[1]


def solution(mesh):
    fine = Mesh(mesh.devices.reshape(4, 2, 4, 2, 2), ("row",) + AXES)
    placed = P("row", AXES)
    return jax.shard_map(shards, mesh=fine, in_specs=(placed,) * 4, out_specs=placed, check_vma=False)
```

```python
import jax
import jax.numpy as jnp
from jax import lax
from jax.experimental import pallas as pl
from jax.experimental.pallas import tpu as pltpu
from jax.sharding import Mesh, PartitionSpec as P

BLOCK = 64
ROWS = 4
A_SLOTS = 8
A_TILES = A_SLOTS // 2
A_ROWS = 8 + A_TILES * BLOCK
B_SLOTS = 38
B_TILES = B_SLOTS // 2
B_ROWS = 8 + B_TILES * BLOCK
MESSAGES = 8
H_K, H_J0, H_J1, H_L0, H_R0, H_L1, H_R1, H_COUNT = range(8)
E_STRIDE = 44
UNROLL = 6
UNPACK = 4
A_SHARDS = 32
A_PER_GROUP = 4
GROUPS = 96
TAB = 1024
TAB_GROUP, TAB_GROUPS, TAB_ROW = 0, 64, 128
C_TILES = 17 * 8
DUMP = 16 * 8
AXES = ("zl", "y", "zh", "core")
F32, BF16, I32 = jnp.float32, jnp.bfloat16, jnp.int32


def _cost(us):
    return pl.CostEstimate(flops=0, transcendentals=0, bytes_accessed=us * 3_690_000)


def _lane(rows=1):
    return lax.broadcasted_iota(I32, (rows, 128), 1)


def _side_by_side(left, right, odd_left, odd_right, keep=None):
    left, right = left.reshape(8, 8, 128), right.reshape(8, 8, 128)
    lane = lax.broadcasted_iota(I32, (1, 8, 128), 2)
    low = lane < 64
    turned = jnp.where(low, odd_left, 1 - odd_right) == 1
    far = pltpu.roll(jnp.where(low, right, left), 64, 2)
    both = jnp.where(turned, far, jnp.where(low, left, right))
    if keep is not None:
        both = jnp.where(jnp.logical_and(lane >= keep[0], lane < keep[1]), both, 0.0)
    return both.reshape(BLOCK, 128)


def pack_a_kernel(mask_ref, a_ref, out_ref, stored):
    shard = lax.axis_index("zl") * 16 + lax.axis_index("y") * 4 + lax.axis_index("zh") * 2 + lax.axis_index("core")
    for s in range(A_SLOTS):
        stored[s] = 0
    n = 0
    counts = []
    for k in range(2):
        for i in range(16):
            stored[n] = k * 16 + i
            n = n + mask_ref[k, i]
        counts.append(n)
    lane = _lane(8)
    head = jnp.where(lane == 8, counts[0], jnp.where(lane == 9, counts[1] - counts[0], jnp.where(lane == 10, shard, 0)))
    for t in range(A_TILES):
        e0, e1 = stored[2 * t], stored[2 * t + 1]
        x0 = a_ref[pl.ds(pl.multiple_of((e0 & 15) * BLOCK, BLOCK), BLOCK), :]
        x1 = a_ref[pl.ds(pl.multiple_of((e1 & 15) * BLOCK, BLOCK), BLOCK), :]
        out_ref[8 + t * BLOCK : 8 + (t + 1) * BLOCK, :] = _side_by_side(x0, x1, e0 >> 4, e1 >> 4)
        head = jnp.where(lane == 2 * t, e0 & 15, jnp.where(lane == 2 * t + 1, e1 & 15, head))
    out_ref[0:8, :] = head.astype(F32)


def pack_a(mask_a, a):
    return pl.pallas_call(
        pack_a_kernel,
        in_specs=[pl.BlockSpec(memory_space=pltpu.SMEM), pl.BlockSpec(memory_space=pltpu.VMEM)],
        out_specs=pl.BlockSpec(memory_space=pltpu.VMEM),
        out_shape=jax.ShapeDtypeStruct((A_ROWS, 128), F32),
        scratch_shapes=[pltpu.SMEM((64,), I32)],
        cost_estimate=_cost(2),
        name="pack_a",
    )(mask_a.T, a)


def pack_b_kernel(round_ref, mask_ref, b_hbm, after_ref, out, token, b, heads, source, size, headv, sem):
    copies = []
    for q in range(4):
        part = pl.ds(q * 256, 256)
        copies.append(pltpu.make_async_copy(b_hbm.at[part, :], b.at[part, :], sem.at[q]))
        copies[-1].start()
    row = lax.axis_index("row")
    for m in range(MESSAGES):
        size[m] = 0
        heads[m, H_COUNT, 0] = 0

    def scan_row(k, carry):
        m, e, n = carry
        par = I32(0)
        for j in range(8):
            m0, m1 = mask_ref[k, 2 * j], mask_ref[k, 2 * j + 1]
            count = m0 + m1
            full = n + count > B_SLOTS
            m = m + full.astype(I32)
            e = jnp.where(full, 0, e)
            n = jnp.where(full, 0, n)
            par = jnp.where(full, 0, par)
            at = e - par
            heads[m, H_K, at] = row * 16 + k
            heads[m, H_J0 + par, at] = j
            heads[m, H_J1, at] = j
            heads[m, H_L1, at] = -1
            heads[m, H_R1, at] = -1
            heads[m, H_L0 + 2 * par, at] = jnp.where(m0 == 1, n, -1)
            heads[m, H_R0 + 2 * par, at] = jnp.where(m1 == 1, n + m0, -1)
            source[m, n] = k * 16 + 2 * j
            source[m, n + m0] = k * 16 + 2 * j + 1
            some = jnp.minimum(count, 1)
            n = n + count
            e = e + some * (1 - par)
            par = par ^ some
            size[m] = n
            heads[m, H_COUNT, 0] = e
        return m, e, n

    last, _, _ = lax.fori_loop(0, 16, scan_row, (I32(0), I32(0), I32(0)))
    token[0] = last
    first = round_ref[0] * 2
    head_copies = []
    for half in range(2):
        heads[first + half, H_COUNT, 1] = last + 1
        head_copies.append(pltpu.make_async_copy(heads.at[first + half], headv.at[half], sem.at[4 + half]))
        head_copies[-1].start()
    for copy in copies:
        copy.wait()
    for half in range(2):
        m = first + half
        n = size[m]

        def some(g, carry, m=m, n=n, half=half):
            tiles = []
            for u in range(4):
                t = jnp.minimum(4 * g + u, B_TILES - 1)
                blocks = []
                for e in (source[m, jnp.minimum(2 * t, n - 1)], source[m, jnp.minimum(2 * t + 1, n - 1)]):
                    rows = pl.ds(pl.multiple_of((e >> 4) * BLOCK, BLOCK), BLOCK)
                    blocks.append((b[rows, pl.ds(pl.multiple_of(((e & 15) >> 1) * 128, 128), 128)], e & 1))
                tiles.append((t, _side_by_side(blocks[0][0], blocks[1][0], blocks[0][1], blocks[1][1])))
            for t, tile in tiles:
                out[pl.ds(pl.multiple_of(half * B_ROWS + 8 + t * BLOCK, 8), BLOCK), :] = tile
            return carry

        lax.fori_loop(0, (n + 7) // 8, some, 0)
    for half in range(2):
        head_copies[half].wait()
        out[half * B_ROWS : half * B_ROWS + 8, :] = headv[half].astype(F32)


def pack_b(rnd, mask_b, b, after):
    smem = pl.BlockSpec(memory_space=pltpu.SMEM)
    vmem = pl.BlockSpec(memory_space=pltpu.VMEM)
    return pl.pallas_call(
        pack_b_kernel,
        in_specs=[smem, smem, pl.BlockSpec(memory_space=pl.ANY), pl.BlockSpec(memory_space=pl.ANY)],
        out_specs=[vmem, smem],
        out_shape=[jax.ShapeDtypeStruct((2 * B_ROWS, 128), F32), jax.ShapeDtypeStruct((1,), I32)],
        scratch_shapes=[
            pltpu.VMEM(b.shape, F32),
            pltpu.SMEM((MESSAGES, 8, 128), I32),
            pltpu.SMEM((MESSAGES, 128), I32),
            pltpu.SMEM((MESSAGES,), I32),
            pltpu.VMEM((2, 8, 128), I32),
            pltpu.SemaphoreType.DMA((6,)),
        ],
        compiler_params=pltpu.CompilerParams(vmem_limit_bytes=8 << 20),
        cost_estimate=_cost(6),
        name="pack_b",
    )(rnd, mask_b, b, after)


def _halves(x):
    hi = x.astype(BF16).astype(F32)
    return hi, x - hi


def unpack_a_kernel(*refs):
    n_a = A_SHARDS // A_PER_GROUP
    a_refs, refs = refs[:n_a], refs[n_a + 1 :]
    lhs, tab, token, ahead, aheadv, sem = refs
    for g in range(n_a):
        for q in range(A_PER_GROUP):
            aheadv[g * A_PER_GROUP + q : g * A_PER_GROUP + q + 1, :] = a_refs[g][q * A_ROWS : q * A_ROWS + 1, :].astype(I32)
    a_head_copy = pltpu.make_async_copy(aheadv, ahead, sem)
    a_head_copy.start()
    a_head_copy.wait()
    low = _lane(BLOCK) < 64
    group = I32(0)
    for g in range(n_a):

        def shard(r, group, g=g):
            q = g * A_PER_GROUP + r
            n0, n1, at = ahead[q, 8], ahead[q, 9], ahead[q, 10]
            g0, g1 = (n0 + 3) >> 2, (n1 + 3) >> 2
            tab[TAB_GROUP + 2 * at] = group
            tab[TAB_GROUP + 2 * at + 1] = group + g0
            tab[TAB_GROUPS + 2 * at] = g0
            tab[TAB_GROUPS + 2 * at + 1] = g1
            for s in range(12):
                tab[TAB_ROW + 4 * group + s] = DUMP
            tiles = []
            for t in range(A_TILES):
                x = a_refs[g][pl.ds(pl.multiple_of(r * A_ROWS + 8 + t * BLOCK, 8), BLOCK), :]
                swapped = pltpu.roll(x, 64, 1)
                for p in range(2):
                    hi, lo = _halves(jnp.where(low, x, swapped) if p == 0 else jnp.where(low, swapped, x))
                    tiles.append(jnp.where(low, hi, lo).astype(BF16))
            for s in range(A_SLOTS):
                place = 4 * group + s + jnp.where(s < n0, 0, 4 * g0 - n0)
                place = jnp.where(s < n0 + n1, place, 4 * GROUPS)
                tab[TAB_ROW + place] = ahead[q, s] * 8
                lhs[pl.ds(pl.multiple_of(place * BLOCK, BLOCK), BLOCK), :] = tiles[s]
            return group + g0 + g1

        group = lax.fori_loop(0, A_PER_GROUP, shard, group)
    for s in range(4):
        tab[TAB_ROW + 4 * GROUPS + s] = DUMP
    token[0] = group


def unpack_a(a_parts, token):
    smem = pl.BlockSpec(memory_space=pltpu.SMEM)
    vmem = pl.BlockSpec(memory_space=pltpu.VMEM)
    return pl.pallas_call(
        unpack_a_kernel,
        in_specs=[vmem] * len(a_parts) + [smem],
        out_specs=[vmem, smem, smem],
        out_shape=[
            jax.ShapeDtypeStruct((4 * (GROUPS + 1) * BLOCK, 128), BF16),
            jax.ShapeDtypeStruct((TAB,), I32),
            jax.ShapeDtypeStruct((1,), I32),
        ],
        scratch_shapes=[pltpu.SMEM((A_SHARDS, 128), I32), pltpu.VMEM((A_SHARDS, 128), I32), pltpu.SemaphoreType.DMA],
        compiler_params=pltpu.CompilerParams(vmem_limit_bytes=16 << 20),
        cost_estimate=_cost(6),
        name="unpack_a",
    )(*a_parts, token)


def product_kernel(*refs, held, first, last):
    n_half = sum(held)
    lhs_hbm, tab, _, refs = refs[0], refs[1], refs[2], refs[3:]
    b_refs, refs = refs[: len(held)], refs[len(held) :]
    b_refs = [ref.at[pl.ds(B_ROWS * q, B_ROWS), :] for ref, n in zip(b_refs, held) for q in range(n)]
    c, refs = refs[0], refs[1:]
    if last:
        c_out, refs = refs[0], refs[1:]
    most_out, bhead, bheadv, rhs, wg, we, wj0, wj1, lhs, sem = refs
    lhs_copy = pltpu.make_async_copy(lhs_hbm, lhs, sem.at[1])
    lhs_copy.start()

    for h in range(n_half):
        bheadv[h] = b_refs[h][0:8, :].astype(I32)
    b_head_copy = pltpu.make_async_copy(bheadv, bhead, sem.at[0])
    b_head_copy.start()
    if first:
        c[...] = jnp.zeros(c.shape, F32)
    b_head_copy.wait()
    most = I32(0)
    work = I32(0)
    for h in range(n_half):
        head, body = bhead.at[h], b_refs[h]
        n = head[H_COUNT, 0]
        most = jnp.maximum(most, head[H_COUNT, 1])

        def unpack(m, w, h=h, head=head, body=body, n=n):
            tiles = []
            for u in range(UNPACK):
                at = jnp.minimum(UNPACK * m + u, n - 1)
                for hl, hr in ((H_L0, H_R0), (H_L1, H_R1)):
                    left, right = head[hl, at], head[hr, at]
                    from_lane = jnp.where(left < 0, 64, 0)
                    to_lane = jnp.where(right < 0, 64, 128)
                    left, right = jnp.maximum(left, 0), jnp.maximum(right, 0)
                    xl = body[pl.ds(pl.multiple_of(8 + (left >> 1) * BLOCK, 8), BLOCK), :]
                    xr = body[pl.ds(pl.multiple_of(8 + (right >> 1) * BLOCK, 8), BLOCK), :]
                    v = _side_by_side(xl, xr, left & 1, right & 1, (from_lane, to_lane))
                    hi, lo = _halves(v)
                    tiles.append((hi.astype(BF16), lo.astype(BF16)))
            for u in range(UNPACK):
                t = UNPACK * m + u
                at = jnp.minimum(t, n - 1)
                place = h * E_STRIDE + t
                for p in range(2):
                    for part in range(2):
                        rhs[pl.ds(pl.multiple_of(place * 256 + p * 128 + part * 64, BLOCK), BLOCK), :] = tiles[2 * u + p][part]
                k, j0, j1 = head[H_K, at], head[H_J0, at], head[H_J1, at]
                group, groups = tab[TAB_GROUP + k], tab[TAB_GROUPS + k]
                groups = jnp.where(t < n, groups, 0)
                for extra in range(2):
                    wg[w] = group + extra
                    we[w] = place
                    wj0[w] = j0
                    wj1[w] = j1
                    w = w + (groups > extra).astype(I32)
            return w

        work = lax.fori_loop(0, (n + UNPACK - 1) // UNPACK, unpack, work)
    for u in range(UNROLL):
        wg[work + u] = GROUPS
        we[work + u] = 0
        wj0[work + u] = 0
        wj1[work + u] = 0

    def multiply(m, carry):
        results = []
        for u in range(UNROLL):
            w = UNROLL * m + u
            left = lhs[pl.ds(pl.multiple_of(wg[w] * 256, 256), 256), :]
            both = rhs[pl.ds(pl.multiple_of(we[w] * 256, 256), 256), :]
            cols = []
            for p in range(2):
                hi, lo = both[p * 128 : p * 128 + 64], both[p * 128 + 64 : p * 128 + 128]
                cols.append(jnp.concatenate([hi, hi, lo, lo], axis=0))
            results.append(
                jnp.dot(
                    jnp.concatenate([left, left], axis=1),
                    jnp.concatenate(cols, axis=1),
                    preferred_element_type=F32,
                )
            )
        for u in range(UNROLL):
            w = UNROLL * m + u
            g = wg[w]
            rows = [tab[TAB_ROW + 4 * g + q] for q in range(4)]
            for p, j in enumerate((wj0[w], wj1[w])):
                sums = [c[rows[q] + j] + results[u][q * BLOCK : (q + 1) * BLOCK, p * 128 : (p + 1) * 128] for q in range(4)]
                for q in range(4):
                    c[rows[q] + j] = sums[q]
        return carry

    lhs_copy.wait()
    lax.fori_loop(0, (work + UNROLL - 1) // UNROLL, multiply, 0)
    most_out[0] = most
    if last:
        out_copies = [
            pltpu.make_async_copy(c.at[8 * i + j], c_out.at[pl.ds(i * BLOCK, BLOCK), pl.ds(j * 128, 128)], sem.at[2])
            for i in range(16)
            for j in range(8)
        ]
        for copy in out_copies:
            copy.start()
        pltpu.make_async_copy(c_out, c_out, sem.at[2]).wait()


def product(lhs, tab, c, halves, first=False, last=False):
    held = [x.shape[0] // B_ROWS for x in halves]
    n_half = sum(held)
    smem = pl.BlockSpec(memory_space=pltpu.SMEM)
    vmem = pl.BlockSpec(memory_space=pltpu.VMEM)
    scratch = [
        pltpu.SMEM((n_half, 8, 128), I32),
        pltpu.VMEM((n_half, 8, 128), I32),
        pltpu.VMEM((n_half * E_STRIDE * 256, 128), BF16),
        pltpu.SMEM((1024,), I32),
        pltpu.SMEM((1024,), I32),
        pltpu.SMEM((1024,), I32),
        pltpu.SMEM((1024,), I32),
        pltpu.VMEM(lhs.shape, BF16),
        pltpu.SemaphoreType.DMA((3,)),
    ]
    out_specs, out_shape = [vmem], [jax.ShapeDtypeStruct((C_TILES, BLOCK, 128), F32)]
    args = (lhs, tab, c) + tuple(halves)
    in_specs = [pl.BlockSpec(memory_space=pltpu.HBM), smem, smem if first else vmem] + [vmem] * len(halves)
    aliases = {} if first else {2: 0}
    if last:
        out_specs.append(pl.BlockSpec(memory_space=pltpu.HBM))
        out_shape.append(jax.ShapeDtypeStruct((1024, 1024), F32))
    out_specs.append(smem)
    out_shape.append(jax.ShapeDtypeStruct((1,), I32))

    def kernel(*refs):
        product_kernel(*refs, held=held, first=first, last=last)

    return pl.pallas_call(
        kernel,
        in_specs=in_specs,
        out_specs=out_specs,
        out_shape=out_shape,
        input_output_aliases=aliases,
        scratch_shapes=scratch,
        compiler_params=pltpu.CompilerParams(vmem_limit_bytes=(n_half * 3 + 14) << 20),
        cost_estimate=_cost(8 if last else 20),
        name="product_first" if first else "product_last" if last else "product_more",
    )(*args)


def _flat(zl, y, zh, core):
    return ((zl * 4 + y) * 2 + zh) * 2 + core


def _turn(step, swapped):
    pairs = []
    for z in range(4):
        for y in range(4):
            for core in range(2):
                along_y = (core == 0) != swapped
                to_y, to_z = ((y + step) % 4, z) if along_y else (y, (z + step) % 4)
                pairs.append((_flat(z % 2, y, z // 2, core), _flat(to_z % 2, to_y, to_z // 2, core)))
    return pairs


def gather_a(packed, token):
    near = [packed] + [lax.ppermute(packed, AXES, _turn(s, False)) for s in (1, 3, 2)]
    *near, token = lax.optimization_barrier((*near, token))
    group = jnp.concatenate(near, axis=0)
    mine = [group] + [lax.ppermute(group, AXES, _turn(s, True)) for s in (1, 3, 2)]
    late = lax.optimization_barrier((group, mine[1], mine[2]))[0]
    other = [lax.ppermute(x, "core", [(0, 1), (1, 0)]) for x in mine[1:] + [late]]
    return mine + other, token


UP = [(i, (i + 1) % ROWS) for i in range(ROWS)]
DOWN = [(i, (i - 1) % ROWS) for i in range(ROWS)]


def near_b(p):
    return lax.ppermute(p, "row", UP), lax.ppermute(p, "row", DOWN)


def far_b(above, below):
    return lax.ppermute(above[:B_ROWS], "row", UP), lax.ppermute(below[B_ROWS:], "row", DOWN)


def shards(a_blocks, mask_a, b_blocks, mask_b):
    pa = pack_a(mask_a, a_blocks)
    p, token = pack_b(jnp.zeros((1,), I32), mask_b, b_blocks, pa)
    near = near_b(p)
    a_parts, token = gather_a(pa, token)
    lhs, tab, token = unpack_a(a_parts, token)
    *near, token = lax.optimization_barrier((*near, token))
    far = far_b(*near)
    c, most0 = product(lhs, tab, token, (p, *near), first=True)
    _, out, most1 = product(lhs, tab, c, far, last=True)
    most = jnp.maximum(most0, most1)[0]

    def again(carry):
        r, out = carry
        p, _ = pack_b(r[None], mask_b, b_blocks, pa)
        near = near_b(p)
        far = far_b(*near)
        c = out.reshape(16, BLOCK, 8, 128).transpose(0, 2, 1, 3).reshape(128, BLOCK, 128)
        c = jnp.pad(c, ((0, C_TILES - 128), (0, 0), (0, 0)))
        c, _ = product(lhs, tab, c, (p,) + near[:1])
        return r + 1, product(lhs, tab, c, near[1:] + far, last=True)[1]

    return lax.while_loop(lambda carry: carry[0] * 2 < most, again, (I32(1), out))[1]


def solution(mesh):
    fine = Mesh(mesh.devices.reshape(4, 2, 4, 2, 2), ("row",) + AXES)
    placed = P("row", AXES)
    return jax.shard_map(shards, mesh=fine, in_specs=(placed,) * 4, out_specs=placed, check_vma=False)
```

```python
import jax
import jax.numpy as jnp
from jax import lax
from jax.experimental import pallas as pl
from jax.experimental.pallas import tpu as pltpu
from jax.sharding import Mesh, PartitionSpec as P

BLOCK = 64
ROWS = 4
A_SLOTS = 8
A_TILES = A_SLOTS // 2
A_ROWS = 8 + A_TILES * BLOCK
B_SLOTS = 38
B_TILES = B_SLOTS // 2
B_ROWS = 8 + B_TILES * BLOCK
MESSAGES = 8
H_K, H_J0, H_J1, H_L0, H_R0, H_L1, H_R1, H_COUNT = range(8)
E_STRIDE = 44
UNROLL = 6
UNPACK = 4
A_SHARDS = 32
A_PER_GROUP = 4
GROUPS = 96
TAB = 1024
TAB_GROUP, TAB_GROUPS, TAB_ROW = 0, 64, 128
C_TILES = 17 * 8
DUMP = 16 * 8
AXES = ("zl", "y", "zh", "core")
F32, BF16, I32 = jnp.float32, jnp.bfloat16, jnp.int32


def _cost(us):
    return pl.CostEstimate(flops=0, transcendentals=0, bytes_accessed=us * 3_690_000)


def _lane(rows=1):
    return lax.broadcasted_iota(I32, (rows, 128), 1)


def _side_by_side(left, right, odd_left, odd_right, keep=None):
    left, right = left.reshape(8, 8, 128), right.reshape(8, 8, 128)
    lane = lax.broadcasted_iota(I32, (1, 8, 128), 2)
    low = lane < 64
    turned = jnp.where(low, odd_left, 1 - odd_right) == 1
    far = pltpu.roll(jnp.where(low, right, left), 64, 2)
    both = jnp.where(turned, far, jnp.where(low, left, right))
    if keep is not None:
        both = jnp.where(jnp.logical_and(lane >= keep[0], lane < keep[1]), both, 0.0)
    return both.reshape(BLOCK, 128)


def pack_a_kernel(mask_ref, a_ref, out_ref, stored):
    shard = lax.axis_index("zl") * 16 + lax.axis_index("y") * 4 + lax.axis_index("zh") * 2 + lax.axis_index("core")
    for s in range(A_SLOTS):
        stored[s] = 0
    n = 0
    counts = []
    for k in range(2):
        for i in range(16):
            stored[n] = k * 16 + i
            n = n + mask_ref[k, i]
        counts.append(n)
    lane = _lane(8)
    head = jnp.where(lane == 8, counts[0], jnp.where(lane == 9, counts[1] - counts[0], jnp.where(lane == 10, shard, 0)))
    for t in range(A_TILES):
        e0, e1 = stored[2 * t], stored[2 * t + 1]
        x0 = a_ref[pl.ds(pl.multiple_of((e0 & 15) * BLOCK, BLOCK), BLOCK), :]
        x1 = a_ref[pl.ds(pl.multiple_of((e1 & 15) * BLOCK, BLOCK), BLOCK), :]
        out_ref[8 + t * BLOCK : 8 + (t + 1) * BLOCK, :] = _side_by_side(x0, x1, e0 >> 4, e1 >> 4)
        head = jnp.where(lane == 2 * t, e0 & 15, jnp.where(lane == 2 * t + 1, e1 & 15, head))
    out_ref[0:8, :] = head.astype(F32)


def pack_a(mask_a, a):
    return pl.pallas_call(
        pack_a_kernel,
        in_specs=[pl.BlockSpec(memory_space=pltpu.SMEM), pl.BlockSpec(memory_space=pltpu.VMEM)],
        out_specs=pl.BlockSpec(memory_space=pltpu.VMEM),
        out_shape=jax.ShapeDtypeStruct((A_ROWS, 128), F32),
        scratch_shapes=[pltpu.SMEM((64,), I32)],
        cost_estimate=_cost(2),
        name="pack_a",
    )(mask_a.T, a)


def pack_b_kernel(round_ref, mask_ref, b_hbm, after_ref, out, token, b, heads, source, size, headv, sem):
    copies = []
    for q in range(4):
        part = pl.ds(q * 256, 256)
        copies.append(pltpu.make_async_copy(b_hbm.at[part, :], b.at[part, :], sem.at[q]))
        copies[-1].start()
    row = lax.axis_index("row")
    for m in range(MESSAGES):
        size[m] = 0
        heads[m, H_COUNT, 0] = 0

    def scan_row(k, carry):
        mask = [mask_ref[k, j] for j in range(16)]
        total = mask
        while len(total) > 1:
            total = [x + y for x, y in zip(total[::2], total[1::2])]

        def scan(carry, may_split):
            m, e, n = carry
            par = I32(0)
            for j in range(8):
                m0, m1 = mask[2 * j], mask[2 * j + 1]
                count = m0 + m1
                if may_split:
                    full = n + count > B_SLOTS
                    size[m] = n
                    heads[m, H_COUNT, 0] = e
                    m = m + full.astype(I32)
                    e = jnp.where(full, 0, e)
                    n = jnp.where(full, 0, n)
                    par = jnp.where(full, 0, par)
                some = m0 | m1
                at = e - par
                heads[m, H_K, at] = row * 16 + k
                heads[m, H_J0 + par, at] = j
                heads[m, H_J1, at] = j
                heads[m, H_L1, at] = -1
                heads[m, H_R1, at] = -1
                heads[m, H_L0 + 2 * par, at] = jnp.where(m0 == 1, n, -1)
                heads[m, H_R0 + 2 * par, at] = jnp.where(m1 == 1, n + m0, -1)
                source[m, n] = k * 16 + 2 * j
                source[m, n + m0] = k * 16 + 2 * j + 1
                n = n + count
                par = par ^ some
                e = at + (par | some)
            size[m] = n
            heads[m, H_COUNT, 0] = e
            return m, e, n

        return lax.cond(carry[2] + total[0] > B_SLOTS, lambda c: scan(c, True), lambda c: scan(c, False), carry)

    last, _, _ = lax.fori_loop(0, 16, scan_row, (I32(0), I32(0), I32(0)))
    token[0] = last
    first = round_ref[0] * 2
    head_copies = []
    for half in range(2):
        heads[first + half, H_COUNT, 1] = last + 1
        head_copies.append(pltpu.make_async_copy(heads.at[first + half], headv.at[half], sem.at[4 + half]))
        head_copies[-1].start()
    for copy in copies:
        copy.wait()
    for half in range(2):
        m = first + half
        n = size[m]

        def some(g, carry, m=m, n=n, half=half):
            tiles = []
            for u in range(4):
                t = jnp.minimum(4 * g + u, B_TILES - 1)
                blocks = []
                for e in (source[m, jnp.minimum(2 * t, n - 1)], source[m, jnp.minimum(2 * t + 1, n - 1)]):
                    rows = pl.ds(pl.multiple_of((e >> 4) * BLOCK, BLOCK), BLOCK)
                    blocks.append((b[rows, pl.ds(pl.multiple_of(((e & 15) >> 1) * 128, 128), 128)], e & 1))
                tiles.append((t, _side_by_side(blocks[0][0], blocks[1][0], blocks[0][1], blocks[1][1])))
            for t, tile in tiles:
                out[pl.ds(pl.multiple_of(half * B_ROWS + 8 + t * BLOCK, 8), BLOCK), :] = tile
            return carry

        lax.fori_loop(0, (n + 7) // 8, some, 0)
    for half in range(2):
        head_copies[half].wait()
        out[half * B_ROWS : half * B_ROWS + 8, :] = headv[half].astype(F32)


def pack_b(rnd, mask_b, b, after):
    smem = pl.BlockSpec(memory_space=pltpu.SMEM)
    vmem = pl.BlockSpec(memory_space=pltpu.VMEM)
    return pl.pallas_call(
        pack_b_kernel,
        in_specs=[smem, smem, pl.BlockSpec(memory_space=pl.ANY), pl.BlockSpec(memory_space=pl.ANY)],
        out_specs=[vmem, smem],
        out_shape=[jax.ShapeDtypeStruct((2 * B_ROWS, 128), F32), jax.ShapeDtypeStruct((1,), I32)],
        scratch_shapes=[
            pltpu.VMEM(b.shape, F32),
            pltpu.SMEM((MESSAGES, 8, 128), I32),
            pltpu.SMEM((MESSAGES, 128), I32),
            pltpu.SMEM((MESSAGES,), I32),
            pltpu.VMEM((2, 8, 128), I32),
            pltpu.SemaphoreType.DMA((6,)),
        ],
        compiler_params=pltpu.CompilerParams(vmem_limit_bytes=8 << 20),
        cost_estimate=_cost(6),
        name="pack_b",
    )(rnd, mask_b, b, after)


def _halves(x):
    hi = x.astype(BF16).astype(F32)
    return hi, x - hi


def unpack_a_kernel(*refs):
    n_a = A_SHARDS // A_PER_GROUP
    a_refs, refs = refs[:n_a], refs[n_a + 1 :]
    lhs, tab, token, ahead, aheadv, sem = refs
    for g in range(n_a):
        for q in range(A_PER_GROUP):
            aheadv[g * A_PER_GROUP + q : g * A_PER_GROUP + q + 1, :] = a_refs[g][q * A_ROWS : q * A_ROWS + 1, :].astype(I32)
    a_head_copy = pltpu.make_async_copy(aheadv, ahead, sem)
    a_head_copy.start()
    a_head_copy.wait()
    low = _lane(BLOCK) < 64
    group = I32(0)
    for g in range(n_a):

        def shard(r, group, g=g):
            q = g * A_PER_GROUP + r
            n0, n1, at = ahead[q, 8], ahead[q, 9], ahead[q, 10]
            g0, g1 = (n0 + 3) >> 2, (n1 + 3) >> 2
            tab[TAB_GROUP + 2 * at] = group
            tab[TAB_GROUP + 2 * at + 1] = group + g0
            tab[TAB_GROUPS + 2 * at] = g0
            tab[TAB_GROUPS + 2 * at + 1] = g1
            for s in range(12):
                tab[TAB_ROW + 4 * group + s] = DUMP
            tiles = []
            for t in range(A_TILES):
                x = a_refs[g][pl.ds(pl.multiple_of(r * A_ROWS + 8 + t * BLOCK, 8), BLOCK), :]
                swapped = pltpu.roll(x, 64, 1)
                for p in range(2):
                    hi, lo = _halves(jnp.where(low, x, swapped) if p == 0 else jnp.where(low, swapped, x))
                    tiles.append(jnp.where(low, hi, lo).astype(BF16))
            for s in range(A_SLOTS):
                place = 4 * group + s + jnp.where(s < n0, 0, 4 * g0 - n0)
                place = jnp.where(s < n0 + n1, place, 4 * GROUPS)
                tab[TAB_ROW + place] = ahead[q, s] * 8
                lhs[pl.ds(pl.multiple_of(place * BLOCK, BLOCK), BLOCK), :] = tiles[s]
            return group + g0 + g1

        group = lax.fori_loop(0, A_PER_GROUP, shard, group)
    for s in range(4):
        tab[TAB_ROW + 4 * GROUPS + s] = DUMP
    token[0] = group


def unpack_a(a_parts, token):
    smem = pl.BlockSpec(memory_space=pltpu.SMEM)
    vmem = pl.BlockSpec(memory_space=pltpu.VMEM)
    return pl.pallas_call(
        unpack_a_kernel,
        in_specs=[vmem] * len(a_parts) + [smem],
        out_specs=[vmem, smem, smem],
        out_shape=[
            jax.ShapeDtypeStruct((4 * (GROUPS + 1) * BLOCK, 128), BF16),
            jax.ShapeDtypeStruct((TAB,), I32),
            jax.ShapeDtypeStruct((1,), I32),
        ],
        scratch_shapes=[pltpu.SMEM((A_SHARDS, 128), I32), pltpu.VMEM((A_SHARDS, 128), I32), pltpu.SemaphoreType.DMA],
        compiler_params=pltpu.CompilerParams(vmem_limit_bytes=16 << 20),
        cost_estimate=_cost(6),
        name="unpack_a",
    )(*a_parts, token)


def product_kernel(*refs, held, first, last):
    n_half = sum(held)
    lhs_in, tab, _, refs = refs[0], refs[1], refs[2], refs[3:]
    b_refs, refs = refs[: len(held)], refs[len(held) :]
    b_refs = [ref.at[pl.ds(B_ROWS * q, B_ROWS), :] for ref, n in zip(b_refs, held) for q in range(n)]
    c, refs = refs[0], refs[1:]
    if last:
        c_out, refs = refs[0], refs[1:]
    if last:
        most_out, bhead, bheadv, rhs, wg, we, wj0, wj1, sem = refs
        lhs = lhs_in
    else:
        most_out, bhead, bheadv, rhs, wg, we, wj0, wj1, lhs, sem = refs
        lhs_copy = pltpu.make_async_copy(lhs_in, lhs, sem.at[1])
        lhs_copy.start()

    for h in range(n_half):
        bheadv[h] = b_refs[h][0:8, :].astype(I32)
    b_head_copy = pltpu.make_async_copy(bheadv, bhead, sem.at[0])
    b_head_copy.start()
    if first:
        c[...] = jnp.zeros(c.shape, F32)
    b_head_copy.wait()
    most = I32(0)
    work = I32(0)
    for h in range(n_half):
        head, body = bhead.at[h], b_refs[h]
        n = head[H_COUNT, 0]
        most = jnp.maximum(most, head[H_COUNT, 1])

        def unpack(m, w, h=h, head=head, body=body, n=n):
            tiles = []
            for u in range(UNPACK):
                at = jnp.minimum(UNPACK * m + u, n - 1)
                for hl, hr in ((H_L0, H_R0), (H_L1, H_R1)):
                    left, right = head[hl, at], head[hr, at]
                    from_lane = jnp.where(left < 0, 64, 0)
                    to_lane = jnp.where(right < 0, 64, 128)
                    left, right = jnp.maximum(left, 0), jnp.maximum(right, 0)
                    xl = body[pl.ds(pl.multiple_of(8 + (left >> 1) * BLOCK, 8), BLOCK), :]
                    xr = body[pl.ds(pl.multiple_of(8 + (right >> 1) * BLOCK, 8), BLOCK), :]
                    v = _side_by_side(xl, xr, left & 1, right & 1, (from_lane, to_lane))
                    hi, lo = _halves(v)
                    tiles.append((hi.astype(BF16), lo.astype(BF16)))
            for u in range(UNPACK):
                t = UNPACK * m + u
                at = jnp.minimum(t, n - 1)
                place = h * E_STRIDE + t
                for p in range(2):
                    for part in range(2):
                        rhs[pl.ds(pl.multiple_of(place * 256 + p * 128 + part * 64, BLOCK), BLOCK), :] = tiles[2 * u + p][part]
                k, j0, j1 = head[H_K, at], head[H_J0, at], head[H_J1, at]
                group, groups = tab[TAB_GROUP + k], tab[TAB_GROUPS + k]
                groups = jnp.where(t < n, groups, 0)
                for extra in range(2):
                    wg[w] = group + extra
                    we[w] = place
                    wj0[w] = j0
                    wj1[w] = j1
                    w = w + (groups > extra).astype(I32)
            return w

        work = lax.fori_loop(0, (n + UNPACK - 1) // UNPACK, unpack, work)
    for u in range(UNROLL):
        wg[work + u] = GROUPS
        we[work + u] = 0
        wj0[work + u] = 0
        wj1[work + u] = 0

    def multiply(m, carry):
        results = []
        for u in range(UNROLL):
            w = UNROLL * m + u
            left = lhs[pl.ds(pl.multiple_of(wg[w] * 256, 256), 256), :]
            both = rhs[pl.ds(pl.multiple_of(we[w] * 256, 256), 256), :]
            cols = []
            for p in range(2):
                hi, lo = both[p * 128 : p * 128 + 64], both[p * 128 + 64 : p * 128 + 128]
                cols.append(jnp.concatenate([hi, hi, lo, lo], axis=0))
            results.append(
                jnp.dot(
                    jnp.concatenate([left, left], axis=1),
                    jnp.concatenate(cols, axis=1),
                    preferred_element_type=F32,
                )
            )
        for u in range(UNROLL):
            w = UNROLL * m + u
            g = wg[w]
            rows = [tab[TAB_ROW + 4 * g + q] for q in range(4)]
            for p, j in enumerate((wj0[w], wj1[w])):
                sums = [c[rows[q] + j] + results[u][q * BLOCK : (q + 1) * BLOCK, p * 128 : (p + 1) * 128] for q in range(4)]
                for q in range(4):
                    c[rows[q] + j] = sums[q]
        return carry

    if not last:
        lhs_copy.wait()
    lax.fori_loop(0, (work + UNROLL - 1) // UNROLL, multiply, 0)
    most_out[0] = most
    if last:
        out_copies = [
            pltpu.make_async_copy(c.at[8 * i + j], c_out.at[pl.ds(i * BLOCK, BLOCK), pl.ds(j * 128, 128)], sem.at[2])
            for i in range(16)
            for j in range(8)
        ]
        for copy in out_copies:
            copy.start()
        pltpu.make_async_copy(c_out, c_out, sem.at[2]).wait()


def product(lhs, tab, c, halves, first=False, last=False):
    held = [x.shape[0] // B_ROWS for x in halves]
    n_half = sum(held)
    smem = pl.BlockSpec(memory_space=pltpu.SMEM)
    vmem = pl.BlockSpec(memory_space=pltpu.VMEM)
    scratch = [
        pltpu.SMEM((n_half, 8, 128), I32),
        pltpu.VMEM((n_half, 8, 128), I32),
        pltpu.VMEM((n_half * E_STRIDE * 256, 128), BF16),
        pltpu.SMEM((1024,), I32),
        pltpu.SMEM((1024,), I32),
        pltpu.SMEM((1024,), I32),
        pltpu.SMEM((1024,), I32),
        *([] if last else [pltpu.VMEM(lhs.shape, BF16)]),
        pltpu.SemaphoreType.DMA((3,)),
    ]
    out_specs, out_shape = [vmem], [jax.ShapeDtypeStruct((C_TILES, BLOCK, 128), F32)]
    args = (lhs, tab, c) + tuple(halves)
    in_specs = [vmem if last else pl.BlockSpec(memory_space=pltpu.HBM), smem, smem if first else vmem] + [vmem] * len(halves)
    aliases = {} if first else {2: 0}
    if last:
        out_specs.append(pl.BlockSpec(memory_space=pltpu.HBM))
        out_shape.append(jax.ShapeDtypeStruct((1024, 1024), F32))
    out_specs.append(smem)
    out_shape.append(jax.ShapeDtypeStruct((1,), I32))

    def kernel(*refs):
        product_kernel(*refs, held=held, first=first, last=last)

    return pl.pallas_call(
        kernel,
        in_specs=in_specs,
        out_specs=out_specs,
        out_shape=out_shape,
        input_output_aliases=aliases,
        scratch_shapes=scratch,
        compiler_params=pltpu.CompilerParams(vmem_limit_bytes=(n_half * 3 + 14) << 20),
        cost_estimate=_cost(8 if last else 20),
        name="product_first" if first else "product_last" if last else "product_more",
    )(*args)


def _flat(zl, y, zh, core):
    return ((zl * 4 + y) * 2 + zh) * 2 + core


def _turn(step, swapped):
    pairs = []
    for z in range(4):
        for y in range(4):
            for core in range(2):
                along_y = (core == 0) != swapped
                to_y, to_z = ((y + step) % 4, z) if along_y else (y, (z + step) % 4)
                pairs.append((_flat(z % 2, y, z // 2, core), _flat(to_z % 2, to_y, to_z // 2, core)))
    return pairs


def gather_a(packed, token):
    near = [packed] + [lax.ppermute(packed, AXES, _turn(s, False)) for s in (1, 3, 2)]
    *near, token = lax.optimization_barrier((*near, token))
    group = jnp.concatenate(near, axis=0)
    mine = [group] + [lax.ppermute(group, AXES, _turn(s, True)) for s in (1, 3, 2)]
    late = lax.optimization_barrier((group, mine[1], mine[2]))[0]
    other = [lax.ppermute(x, "core", [(0, 1), (1, 0)]) for x in mine[1:] + [late]]
    return mine + other, token


UP = [(i, (i + 1) % ROWS) for i in range(ROWS)]
DOWN = [(i, (i - 1) % ROWS) for i in range(ROWS)]


def near_b(p):
    return lax.ppermute(p, "row", UP), lax.ppermute(p, "row", DOWN)


def far_b(above, below):
    return lax.ppermute(above[:B_ROWS], "row", UP), lax.ppermute(below[B_ROWS:], "row", DOWN)


def shards(a_blocks, mask_a, b_blocks, mask_b):
    pa = pack_a(mask_a, a_blocks)
    p, token = pack_b(jnp.zeros((1,), I32), mask_b, b_blocks, pa)
    near = near_b(p)
    a_parts, token = gather_a(pa, token)
    lhs, tab, token = unpack_a(a_parts, token)
    *near, token = lax.optimization_barrier((*near, token))
    far = far_b(*near)
    c, most0 = product(lhs, tab, token, (p, *near), first=True)
    _, out, most1 = product(lhs, tab, c, far, last=True)
    most = jnp.maximum(most0, most1)[0]

    def again(carry):
        r, out = carry
        p, _ = pack_b(r[None], mask_b, b_blocks, pa)
        near = near_b(p)
        far = far_b(*near)
        c = out.reshape(16, BLOCK, 8, 128).transpose(0, 2, 1, 3).reshape(128, BLOCK, 128)
        c = jnp.pad(c, ((0, C_TILES - 128), (0, 0), (0, 0)))
        c, _ = product(lhs, tab, c, (p,) + near[:1])
        return r + 1, product(lhs, tab, c, near[1:] + far, last=True)[1]

    return lax.while_loop(lambda carry: carry[0] * 2 < most, again, (I32(1), out))[1]


def solution(mesh):
    fine = Mesh(mesh.devices.reshape(4, 2, 4, 2, 2), ("row",) + AXES)
    placed = P("row", AXES)
    return jax.shard_map(shards, mesh=fine, in_specs=(placed,) * 4, out_specs=placed, check_vma=False)
```

```python
import jax
import jax.numpy as jnp
from jax import lax
from jax.experimental import pallas as pl
from jax.experimental.pallas import tpu as pltpu
from jax.sharding import Mesh, PartitionSpec as P

BLOCK = 64
ROWS = 4
A_SLOTS = 8
A_TILES = A_SLOTS // 2
A_ROWS = 8 + A_TILES * BLOCK
B_SLOTS = 38
B_TILES = B_SLOTS // 2
B_ROWS = 8 + B_TILES * BLOCK
MESSAGES = 8
H_K, H_J0, H_J1, H_L0, H_R0, H_L1, H_R1, H_COUNT = range(8)
E_STRIDE = 44
UNROLL = 8
UNPACK = 4
A_SHARDS = 32
A_PER_GROUP = 4
GROUPS = 96
TAB = 1024
TAB_GROUP, TAB_GROUPS, TAB_ROW = 0, 64, 128
C_TILES = 17 * 8
DUMP = 16 * 8
AXES = ("zl", "y", "zh", "core")
F32, BF16, I32 = jnp.float32, jnp.bfloat16, jnp.int32


def _cost(us):
    return pl.CostEstimate(flops=0, transcendentals=0, bytes_accessed=us * 3_690_000)


def _lane(rows=1):
    return lax.broadcasted_iota(I32, (rows, 128), 1)


def _side_by_side(left, right, odd_left, odd_right, keep=None):
    left, right = left.reshape(8, 8, 128), right.reshape(8, 8, 128)
    lane = lax.broadcasted_iota(I32, (1, 8, 128), 2)
    low = lane < 64
    turned = jnp.where(low, odd_left, 1 - odd_right) == 1
    far = pltpu.roll(jnp.where(low, right, left), 64, 2)
    both = jnp.where(turned, far, jnp.where(low, left, right))
    if keep is not None:
        both = jnp.where(jnp.logical_and(lane >= keep[0], lane < keep[1]), both, 0.0)
    return both.reshape(BLOCK, 128)


def pack_a_kernel(mask_ref, a_ref, out_ref, stored):
    shard = lax.axis_index("zl") * 16 + lax.axis_index("y") * 4 + lax.axis_index("zh") * 2 + lax.axis_index("core")
    for s in range(A_SLOTS):
        stored[s] = 0
    n = 0
    counts = []
    for k in range(2):
        for i in range(16):
            stored[n] = k * 16 + i
            n = n + mask_ref[k, i]
        counts.append(n)
    lane = _lane(8)
    head = jnp.where(lane == 8, counts[0], jnp.where(lane == 9, counts[1] - counts[0], jnp.where(lane == 10, shard, 0)))
    for t in range(A_TILES):
        e0, e1 = stored[2 * t], stored[2 * t + 1]
        x0 = a_ref[pl.ds(pl.multiple_of((e0 & 15) * BLOCK, BLOCK), BLOCK), :]
        x1 = a_ref[pl.ds(pl.multiple_of((e1 & 15) * BLOCK, BLOCK), BLOCK), :]
        out_ref[8 + t * BLOCK : 8 + (t + 1) * BLOCK, :] = _side_by_side(x0, x1, e0 >> 4, e1 >> 4)
        head = jnp.where(lane == 2 * t, e0 & 15, jnp.where(lane == 2 * t + 1, e1 & 15, head))
    out_ref[0:8, :] = head.astype(F32)


def pack_a(mask_a, a):
    return pl.pallas_call(
        pack_a_kernel,
        in_specs=[pl.BlockSpec(memory_space=pltpu.SMEM), pl.BlockSpec(memory_space=pltpu.VMEM)],
        out_specs=pl.BlockSpec(memory_space=pltpu.VMEM),
        out_shape=jax.ShapeDtypeStruct((A_ROWS, 128), F32),
        scratch_shapes=[pltpu.SMEM((64,), I32)],
        cost_estimate=_cost(2),
        name="pack_a",
    )(mask_a.T, a)


def pack_b_kernel(round_ref, mask_ref, b_hbm, after_ref, out, token, b, heads, source, size, headv, sem):
    copies = []
    for q in range(4):
        part = pl.ds(q * 256, 256)
        copies.append(pltpu.make_async_copy(b_hbm.at[part, :], b.at[part, :], sem.at[q]))
        copies[-1].start()
    row = lax.axis_index("row")
    for m in range(MESSAGES):
        size[m] = 0
        heads[m, H_COUNT, 0] = 0

    def scan_row(k, carry):
        mask = [mask_ref[k, j] for j in range(16)]
        total = mask
        while len(total) > 1:
            total = [x + y for x, y in zip(total[::2], total[1::2])]

        def scan(carry, may_split):
            m, e, n = carry
            par = I32(0)
            for j in range(8):
                m0, m1 = mask[2 * j], mask[2 * j + 1]
                count = m0 + m1
                if may_split:
                    full = n + count > B_SLOTS
                    size[m] = n
                    heads[m, H_COUNT, 0] = e
                    m = m + full.astype(I32)
                    e = jnp.where(full, 0, e)
                    n = jnp.where(full, 0, n)
                    par = jnp.where(full, 0, par)
                some = m0 | m1
                at = e - par
                heads[m, H_K, at] = row * 16 + k
                heads[m, H_J0 + par, at] = j
                heads[m, H_J1, at] = j
                heads[m, H_L1, at] = -1
                heads[m, H_R1, at] = -1
                heads[m, H_L0 + 2 * par, at] = jnp.where(m0 == 1, n, -1)
                heads[m, H_R0 + 2 * par, at] = jnp.where(m1 == 1, n + m0, -1)
                source[m, n] = k * 16 + 2 * j
                source[m, n + m0] = k * 16 + 2 * j + 1
                n = n + count
                par = par ^ some
                e = at + (par | some)
            size[m] = n
            heads[m, H_COUNT, 0] = e
            return m, e, n

        return lax.cond(carry[2] + total[0] > B_SLOTS, lambda c: scan(c, True), lambda c: scan(c, False), carry)

    last, _, _ = lax.fori_loop(0, 16, scan_row, (I32(0), I32(0), I32(0)))
    token[0] = last
    first = round_ref[0] * 2
    head_copies = []
    for half in range(2):
        heads[first + half, H_COUNT, 1] = last + 1
        head_copies.append(pltpu.make_async_copy(heads.at[first + half], headv.at[half], sem.at[4 + half]))
        head_copies[-1].start()
    for copy in copies:
        copy.wait()
    for half in range(2):
        m = first + half
        n = size[m]

        def some(g, carry, m=m, n=n, half=half):
            tiles = []
            for u in range(4):
                t = jnp.minimum(4 * g + u, B_TILES - 1)
                blocks = []
                for e in (source[m, jnp.minimum(2 * t, n - 1)], source[m, jnp.minimum(2 * t + 1, n - 1)]):
                    rows = pl.ds(pl.multiple_of((e >> 4) * BLOCK, BLOCK), BLOCK)
                    blocks.append((b[rows, pl.ds(pl.multiple_of(((e & 15) >> 1) * 128, 128), 128)], e & 1))
                tiles.append((t, _side_by_side(blocks[0][0], blocks[1][0], blocks[0][1], blocks[1][1])))
            for t, tile in tiles:
                out[pl.ds(pl.multiple_of(half * B_ROWS + 8 + t * BLOCK, 8), BLOCK), :] = tile
            return carry

        lax.fori_loop(0, (n + 7) // 8, some, 0)
    for half in range(2):
        head_copies[half].wait()
        out[half * B_ROWS : half * B_ROWS + 8, :] = headv[half].astype(F32)


def pack_b(rnd, mask_b, b, after):
    smem = pl.BlockSpec(memory_space=pltpu.SMEM)
    vmem = pl.BlockSpec(memory_space=pltpu.VMEM)
    return pl.pallas_call(
        pack_b_kernel,
        in_specs=[smem, smem, pl.BlockSpec(memory_space=pl.ANY), pl.BlockSpec(memory_space=pl.ANY)],
        out_specs=[vmem, smem],
        out_shape=[jax.ShapeDtypeStruct((2 * B_ROWS, 128), F32), jax.ShapeDtypeStruct((1,), I32)],
        scratch_shapes=[
            pltpu.VMEM(b.shape, F32),
            pltpu.SMEM((MESSAGES, 8, 128), I32),
            pltpu.SMEM((MESSAGES, 128), I32),
            pltpu.SMEM((MESSAGES,), I32),
            pltpu.VMEM((2, 8, 128), I32),
            pltpu.SemaphoreType.DMA((6,)),
        ],
        compiler_params=pltpu.CompilerParams(vmem_limit_bytes=8 << 20),
        cost_estimate=_cost(6),
        name="pack_b",
    )(rnd, mask_b, b, after)


def _halves(x):
    hi = x.astype(BF16).astype(F32)
    return hi, x - hi


def unpack_a_kernel(*refs):
    n_a = A_SHARDS // A_PER_GROUP
    a_refs, refs = refs[:n_a], refs[n_a + 1 :]
    lhs, tab, token, ahead, aheadv, sem = refs
    for g in range(n_a):
        for q in range(A_PER_GROUP):
            aheadv[g * A_PER_GROUP + q : g * A_PER_GROUP + q + 1, :] = a_refs[g][q * A_ROWS : q * A_ROWS + 1, :].astype(I32)
    a_head_copy = pltpu.make_async_copy(aheadv, ahead, sem)
    a_head_copy.start()
    a_head_copy.wait()
    low = _lane(BLOCK) < 64
    group = I32(0)
    for g in range(n_a):

        def shard(r, group, g=g):
            q = g * A_PER_GROUP + r
            n0, n1, at = ahead[q, 8], ahead[q, 9], ahead[q, 10]
            g0, g1 = (n0 + 3) >> 2, (n1 + 3) >> 2
            tab[TAB_GROUP + 2 * at] = group
            tab[TAB_GROUP + 2 * at + 1] = group + g0
            tab[TAB_GROUPS + 2 * at] = g0
            tab[TAB_GROUPS + 2 * at + 1] = g1
            for s in range(12):
                tab[TAB_ROW + 4 * group + s] = DUMP
            tiles = []
            for t in range(A_TILES):
                x = a_refs[g][pl.ds(pl.multiple_of(r * A_ROWS + 8 + t * BLOCK, 8), BLOCK), :]
                swapped = pltpu.roll(x, 64, 1)
                for p in range(2):
                    hi, lo = _halves(jnp.where(low, x, swapped) if p == 0 else jnp.where(low, swapped, x))
                    tiles.append(jnp.where(low, hi, lo).astype(BF16))
            for s in range(A_SLOTS):
                place = 4 * group + s + jnp.where(s < n0, 0, 4 * g0 - n0)
                place = jnp.where(s < n0 + n1, place, 4 * GROUPS)
                tab[TAB_ROW + place] = ahead[q, s] * 8
                lhs[pl.ds(pl.multiple_of(place * BLOCK, BLOCK), BLOCK), :] = tiles[s]
            return group + g0 + g1

        group = lax.fori_loop(0, A_PER_GROUP, shard, group)
    for s in range(4):
        tab[TAB_ROW + 4 * GROUPS + s] = DUMP
    token[0] = group


def unpack_a(a_parts, token):
    smem = pl.BlockSpec(memory_space=pltpu.SMEM)
    vmem = pl.BlockSpec(memory_space=pltpu.VMEM)
    return pl.pallas_call(
        unpack_a_kernel,
        in_specs=[vmem] * len(a_parts) + [smem],
        out_specs=[vmem, smem, smem],
        out_shape=[
            jax.ShapeDtypeStruct((4 * (GROUPS + 1) * BLOCK, 128), BF16),
            jax.ShapeDtypeStruct((TAB,), I32),
            jax.ShapeDtypeStruct((1,), I32),
        ],
        scratch_shapes=[pltpu.SMEM((A_SHARDS, 128), I32), pltpu.VMEM((A_SHARDS, 128), I32), pltpu.SemaphoreType.DMA],
        compiler_params=pltpu.CompilerParams(vmem_limit_bytes=16 << 20),
        cost_estimate=_cost(6),
        name="unpack_a",
    )(*a_parts, token)


def product_kernel(*refs, held, first, last):
    n_half = sum(held)
    lhs_in, tab, _, refs = refs[0], refs[1], refs[2], refs[3:]
    b_refs, refs = refs[: len(held)], refs[len(held) :]
    b_refs = [ref.at[pl.ds(B_ROWS * q, B_ROWS), :] for ref, n in zip(b_refs, held) for q in range(n)]
    c, refs = refs[0], refs[1:]
    if last:
        c_out, refs = refs[0], refs[1:]
    if last:
        most_out, bhead, bheadv, rhs, wg, we, wj0, wj1, sem = refs
        lhs = lhs_in
    else:
        most_out, bhead, bheadv, rhs, wg, we, wj0, wj1, lhs, sem = refs
        lhs_copy = pltpu.make_async_copy(lhs_in, lhs, sem.at[1])
        lhs_copy.start()

    for h in range(n_half):
        bheadv[h] = b_refs[h][0:8, :].astype(I32)
    b_head_copy = pltpu.make_async_copy(bheadv, bhead, sem.at[0])
    b_head_copy.start()
    if first:
        c[...] = jnp.zeros(c.shape, F32)
    b_head_copy.wait()
    most = I32(0)
    work = I32(0)
    for h in range(n_half):
        head, body = bhead.at[h], b_refs[h]
        n = head[H_COUNT, 0]
        most = jnp.maximum(most, head[H_COUNT, 1])

        def unpack(m, w, h=h, head=head, body=body, n=n):
            tiles = []
            for u in range(UNPACK):
                at = jnp.minimum(UNPACK * m + u, n - 1)
                for hl, hr in ((H_L0, H_R0), (H_L1, H_R1)):
                    left, right = head[hl, at], head[hr, at]
                    from_lane = jnp.where(left < 0, 64, 0)
                    to_lane = jnp.where(right < 0, 64, 128)
                    left, right = jnp.maximum(left, 0), jnp.maximum(right, 0)
                    xl = body[pl.ds(pl.multiple_of(8 + (left >> 1) * BLOCK, 8), BLOCK), :]
                    xr = body[pl.ds(pl.multiple_of(8 + (right >> 1) * BLOCK, 8), BLOCK), :]
                    v = _side_by_side(xl, xr, left & 1, right & 1, (from_lane, to_lane))
                    hi, lo = _halves(v)
                    tiles.append((hi.astype(BF16), lo.astype(BF16)))
            for u in range(UNPACK):
                t = UNPACK * m + u
                at = jnp.minimum(t, n - 1)
                place = h * E_STRIDE + t
                for p in range(2):
                    for part in range(2):
                        rhs[pl.ds(pl.multiple_of(place * 256 + p * 128 + part * 64, BLOCK), BLOCK), :] = tiles[2 * u + p][part]
                k, j0, j1 = head[H_K, at], head[H_J0, at], head[H_J1, at]
                group, groups = tab[TAB_GROUP + k], tab[TAB_GROUPS + k]
                groups = jnp.where(t < n, groups, 0)
                for extra in range(2):
                    wg[w] = group + extra
                    we[w] = place
                    wj0[w] = j0
                    wj1[w] = j1
                    w = w + (groups > extra).astype(I32)
            return w

        work = lax.fori_loop(0, (n + UNPACK - 1) // UNPACK, unpack, work)
    for u in range(UNROLL):
        wg[work + u] = GROUPS
        we[work + u] = 0
        wj0[work + u] = 0
        wj1[work + u] = 0

    def multiply(m, carry):
        results = []
        for u in range(UNROLL):
            w = UNROLL * m + u
            left = lhs[pl.ds(pl.multiple_of(wg[w] * 256, 256), 256), :]
            both = rhs[pl.ds(pl.multiple_of(we[w] * 256, 256), 256), :]
            cols = []
            for p in range(2):
                hi, lo = both[p * 128 : p * 128 + 64], both[p * 128 + 64 : p * 128 + 128]
                cols.append(jnp.concatenate([hi, hi, lo, lo], axis=0))
            results.append(
                jnp.dot(
                    jnp.concatenate([left, left], axis=1),
                    jnp.concatenate(cols, axis=1),
                    preferred_element_type=F32,
                )
            )
        for u in range(UNROLL):
            w = UNROLL * m + u
            g = wg[w]
            rows = [tab[TAB_ROW + 4 * g + q] for q in range(4)]
            for p, j in enumerate((wj0[w], wj1[w])):
                sums = [c[rows[q] + j] + results[u][q * BLOCK : (q + 1) * BLOCK, p * 128 : (p + 1) * 128] for q in range(4)]
                for q in range(4):
                    c[rows[q] + j] = sums[q]
        return carry

    if not last:
        lhs_copy.wait()
    lax.fori_loop(0, (work + UNROLL - 1) // UNROLL, multiply, 0)
    most_out[0] = most
    if last:
        out_copies = [
            pltpu.make_async_copy(c.at[8 * i + j], c_out.at[pl.ds(i * BLOCK, BLOCK), pl.ds(j * 128, 128)], sem.at[2])
            for i in range(16)
            for j in range(8)
        ]
        for copy in out_copies:
            copy.start()
        pltpu.make_async_copy(c_out, c_out, sem.at[2]).wait()


def product(lhs, tab, c, halves, first=False, last=False):
    held = [x.shape[0] // B_ROWS for x in halves]
    n_half = sum(held)
    smem = pl.BlockSpec(memory_space=pltpu.SMEM)
    vmem = pl.BlockSpec(memory_space=pltpu.VMEM)
    scratch = [
        pltpu.SMEM((n_half, 8, 128), I32),
        pltpu.VMEM((n_half, 8, 128), I32),
        pltpu.VMEM((n_half * E_STRIDE * 256, 128), BF16),
        pltpu.SMEM((1024,), I32),
        pltpu.SMEM((1024,), I32),
        pltpu.SMEM((1024,), I32),
        pltpu.SMEM((1024,), I32),
        *([] if last else [pltpu.VMEM(lhs.shape, BF16)]),
        pltpu.SemaphoreType.DMA((3,)),
    ]
    out_specs, out_shape = [vmem], [jax.ShapeDtypeStruct((C_TILES, BLOCK, 128), F32)]
    args = (lhs, tab, c) + tuple(halves)
    in_specs = [vmem if last else pl.BlockSpec(memory_space=pltpu.HBM), smem, smem if first else vmem] + [vmem] * len(halves)
    aliases = {} if first else {2: 0}
    if last:
        out_specs.append(pl.BlockSpec(memory_space=pltpu.HBM))
        out_shape.append(jax.ShapeDtypeStruct((1024, 1024), F32))
    out_specs.append(smem)
    out_shape.append(jax.ShapeDtypeStruct((1,), I32))

    def kernel(*refs):
        product_kernel(*refs, held=held, first=first, last=last)

    return pl.pallas_call(
        kernel,
        in_specs=in_specs,
        out_specs=out_specs,
        out_shape=out_shape,
        input_output_aliases=aliases,
        scratch_shapes=scratch,
        compiler_params=pltpu.CompilerParams(vmem_limit_bytes=(n_half * 3 + 14) << 20),
        cost_estimate=_cost(8 if last else 20),
        name="product_first" if first else "product_last" if last else "product_more",
    )(*args)


def _flat(zl, y, zh, core):
    return ((zl * 4 + y) * 2 + zh) * 2 + core


def _turn(step, swapped):
    pairs = []
    for z in range(4):
        for y in range(4):
            for core in range(2):
                along_y = (core == 0) != swapped
                to_y, to_z = ((y + step) % 4, z) if along_y else (y, (z + step) % 4)
                pairs.append((_flat(z % 2, y, z // 2, core), _flat(to_z % 2, to_y, to_z // 2, core)))
    return pairs


def gather_a(packed, token):
    near = [packed] + [lax.ppermute(packed, AXES, _turn(s, False)) for s in (1, 3, 2)]
    *near, token = lax.optimization_barrier((*near, token))
    group = jnp.concatenate(near, axis=0)
    mine = [group] + [lax.ppermute(group, AXES, _turn(s, True)) for s in (1, 3, 2)]
    late = lax.optimization_barrier((group, mine[1], mine[2]))[0]
    other = [lax.ppermute(x, "core", [(0, 1), (1, 0)]) for x in mine[1:] + [late]]
    return mine + other, token


UP = [(i, (i + 1) % ROWS) for i in range(ROWS)]
DOWN = [(i, (i - 1) % ROWS) for i in range(ROWS)]


def near_b(p):
    return lax.ppermute(p, "row", UP), lax.ppermute(p, "row", DOWN)


def far_b(above, below):
    return lax.ppermute(above[:B_ROWS], "row", UP), lax.ppermute(below[B_ROWS:], "row", DOWN)


def shards(a_blocks, mask_a, b_blocks, mask_b):
    pa = pack_a(mask_a, a_blocks)
    p, token = pack_b(jnp.zeros((1,), I32), mask_b, b_blocks, pa)
    near = near_b(p)
    a_parts, token = gather_a(pa, token)
    lhs, tab, token = unpack_a(a_parts, token)
    *near, token = lax.optimization_barrier((*near, token))
    far = far_b(*near)
    c, most0 = product(lhs, tab, token, (p, *near), first=True)
    _, out, most1 = product(lhs, tab, c, far, last=True)
    most = jnp.maximum(most0, most1)[0]

    def again(carry):
        r, out = carry
        p, _ = pack_b(r[None], mask_b, b_blocks, pa)
        near = near_b(p)
        far = far_b(*near)
        c = out.reshape(16, BLOCK, 8, 128).transpose(0, 2, 1, 3).reshape(128, BLOCK, 128)
        c = jnp.pad(c, ((0, C_TILES - 128), (0, 0), (0, 0)))
        c, _ = product(lhs, tab, c, (p,) + near[:1])
        return r + 1, product(lhs, tab, c, near[1:] + far, last=True)[1]

    return lax.while_loop(lambda carry: carry[0] * 2 < most, again, (I32(1), out))[1]


def solution(mesh):
    fine = Mesh(mesh.devices.reshape(4, 2, 4, 2, 2), ("row",) + AXES)
    placed = P("row", AXES)
    return jax.shard_map(shards, mesh=fine, in_specs=(placed,) * 4, out_specs=placed, check_vma=False)
```
